32 devices in a mesh: parts: 2 (over y), tp: 4 (over z), sec: 4 (over x, core).
Axes of the slice: x: 2, y: 2, z: 4, core: 2. Of those that a mesh axis runs over, the one named last changes fastest.
Arguments:
- queries: bfloat16 [256, 8192], P(('parts', 'sec', 'tp')), parts along dimension 0, may hold values from -64 to 64
- keys: bfloat16 [256, 256, 1024], P(('parts', 'sec', 'tp')), parts along dimension 0, may hold values from -6 to 6
- values: bfloat16 [256, 256, 1024], P(('parts', 'sec', 'tp')), parts along dimension 0, may hold values from -6 to 6
- lengths: int32 [256], P(('parts', 'sec', 'tp')), parts along dimension 0, may hold values from 2 to 256, as said below
- batch_of_slot: int32 [256], P('parts'), parts along dimension 0, may hold values from 0 to 127, each once
- residual: bfloat16 [256, 8192], P('parts', 'sec'), parts along dimension 0, may hold values from -16 to 16
- out_weight: bfloat16 [8192, 8192], P('tp', 'sec'), may hold values from -0.25 to 0.25
- norm_gain: float32 [8192], P('sec'), may hold values from 0.1 to 1.9
- gate_weight: bfloat16 [8192, 14336], P('sec', 'tp'), may hold values from -0.0625 to 0.0625
- up_weight: bfloat16 [8192, 14336], P('sec', 'tp'), may hold values from -0.0625 to 0.0625
- down_weight: bfloat16 [14336, 8192], P('tp', 'sec'), may hold values from -0.046875 to 0.046875
Outputs:
- layer_out: bfloat16 [256, 8192], P(('parts', 'sec', 'tp')), parts along dimension 0
The draws below stay inside these ranges and needn't reach their ends.
There are 2 independent parts, one for each index of `parts`. The reference program is written for one: setup_inputs(seed, part) draws one part's arguments, and reference() takes and returns one part's arrays. A program takes and returns all parts, laid end to end along the dimension named above; an argument that names none is the same for every part. Nothing has to cross between parts.
Inputs may be any that keep to these rules, and one draw needn't show every extreme that they name: `lengths`: some request has exactly 256 valid positions. `batch_of_slot`: each batch row appears once.
All inputs are finite; a program needn't handle non-finite values.
Results may differ from the reference program's by a relative error of at most 0.0051.
Values may be sent and summed in bfloat16 or wider, within the bound.
A program may use at most 192 MiB of HBM per device.

```python
import math
import jax
import jax.numpy as jnp
from jax import lax

D = 8192
QUERY_HEADS = 64
KEY_VALUE_HEADS = 8
HEAD_WIDTH = 128
FF = 14336
CACHE_LENGTH = 256
REQUEST_COUNT = 128


def query_key_pair(key):
    query_seed = jax.random.fold_in(key, 101)
    cache_random_seed = jax.random.fold_in(key, 102)
    query_vals = jnp.clip(jax.random.normal(query_seed, (REQUEST_COUNT, QUERY_HEADS * HEAD_WIDTH), jnp.float32), -6.0, 6.0)
    key_entries = jnp.clip(jax.random.normal(cache_random_seed, (REQUEST_COUNT, CACHE_LENGTH, KEY_VALUE_HEADS * HEAD_WIDTH), jnp.float32), -6.0, 6.0)
    return (query_vals, key_entries)


def draw_queries(key, part):
    return query_key_pair(key)[0].astype(jnp.bfloat16)


def draw_keys(key, part):
    return query_key_pair(key)[1].astype(jnp.bfloat16)


def draw_residual(key, part):
    column = jnp.arange(D, dtype=jnp.float32) / (D - 1) - 0.5
    base = jax.random.normal(jax.random.fold_in(key, 201), (REQUEST_COUNT, D), jnp.float32)
    drawn = base * jnp.exp(math.log(3.0) * column)
    return jnp.clip(drawn, -16.0, 16.0).astype(jnp.bfloat16)


def draw_lengths(key, part):
    drawn = jax.random.randint(jax.random.fold_in(key, 301), (REQUEST_COUNT,), 2, CACHE_LENGTH + 1)
    chosen_slot = jax.random.randint(jax.random.fold_in(key, 302), (), 0, REQUEST_COUNT)
    return jnp.where(jnp.arange(REQUEST_COUNT) == chosen_slot, CACHE_LENGTH, drawn).astype(jnp.int32)


def block_scale(rng, extent, pieces, least, high):
    def one(axis_at, parts):
        steps = jax.random.uniform(jax.random.fold_in(jax.random.fold_in(rng, 6), axis_at), (parts,), jnp.float32, least / len(pieces), high / len(pieces))
        return jnp.repeat(jnp.exp(steps), extent[axis_at] // parts).reshape((-1,) + (1,) * (len(extent) - axis_at - 1))

    gain = one(*pieces[0])
    for cut in pieces[1:]:
        gain = gain * one(*cut)
    return gain


def bell_draw(rng, extent, deviation, limit, split=(), held_as=jnp.bfloat16):
    values = deviation * jax.random.normal(rng, extent, jnp.float32)
    if split:
        values = values * block_scale(rng, extent, split, -0.22, 0.18)
    return jnp.clip(values, -limit, limit).astype(held_as)


def setup_inputs(seed: int = 0, part: int = 0) -> dict:
    splits = jax.random.split(jax.random.key(seed), 12)
    part_keys = jax.random.split(jax.random.fold_in(splits[11], part), 12)
    queries = draw_queries(jax.random.fold_in(jax.random.fold_in(splits[11], part), 71), part)
    keys = draw_keys(jax.random.fold_in(jax.random.fold_in(splits[11], part), 71), part)
    values = bell_draw(part_keys[2], (REQUEST_COUNT, CACHE_LENGTH, KEY_VALUE_HEADS * HEAD_WIDTH), 1.0, 6.0, ((0, 16),))
    lengths = draw_lengths(jax.random.fold_in(jax.random.fold_in(splits[11], part), 71), part)
    batch_of_slot = jax.random.permutation(part_keys[4], REQUEST_COUNT).astype(jnp.int32)
    residual = draw_residual(jax.random.fold_in(jax.random.fold_in(splits[11], part), 71), part)
    out_weight = bell_draw(splits[6], (QUERY_HEADS * HEAD_WIDTH, D), (QUERY_HEADS * HEAD_WIDTH // 16) ** -0.5, 0.25, ((0, 4), (1, 4)))
    norm_gain = jnp.clip(1.0 + 0.18 * jax.random.normal(splits[7], (D,), jnp.float32), 0.1, 1.9)
    gate_weight = bell_draw(splits[8], (D, FF), D ** -0.5, 0.0625, ((0, 4), (1, 4)))
    up_weight = bell_draw(splits[9], (D, FF), D ** -0.5, 0.0625, ((0, 4), (1, 4)))
    down_weight = bell_draw(splits[10], (FF, D), FF ** -0.5, 0.046875, ((0, 4), (1, 4)))
    return {"queries": queries, "keys": keys, "values": values, "lengths": lengths, "batch_of_slot": batch_of_slot, "residual": residual, "out_weight": out_weight, "norm_gain": norm_gain, "gate_weight": gate_weight, "up_weight": up_weight, "down_weight": down_weight}


def attend_one(inputs):
    query_single, key_lines, value_lines, length = inputs
    group_width = QUERY_HEADS // KEY_VALUE_HEADS
    query_table = query_single.astype(jnp.float32).reshape(KEY_VALUE_HEADS, group_width, HEAD_WIDTH)
    key_table = key_lines.astype(jnp.float32).reshape(CACHE_LENGTH, KEY_VALUE_HEADS, HEAD_WIDTH)
    value_table = value_lines.astype(jnp.float32).reshape(CACHE_LENGTH, KEY_VALUE_HEADS, HEAD_WIDTH)
    scores = jnp.einsum('kgd,pkd->kgp', query_table, key_table) * HEAD_WIDTH ** (-0.5)
    positions = lax.broadcasted_iota(jnp.int32, scores.shape, 2)
    in_cache = positions < length
    scores = jnp.where(in_cache, scores, -jnp.inf)
    row_max = lax.optimization_barrier(jnp.max(scores, axis=2, keepdims=True))
    weights = jnp.exp(scores - row_max)
    probabilities = (weights / lax.optimization_barrier(jnp.sum(weights, axis=2, keepdims=True))).astype(jnp.bfloat16)
    attended = jnp.einsum('kgp,pkd->kgd', probabilities.astype(jnp.float32), value_table)
    return attended.astype(jnp.bfloat16).reshape(QUERY_HEADS * HEAD_WIDTH)

def reference(queries, keys, values, lengths, batch_of_slot, residual, out_weight, norm_gain, gate_weight, up_weight, down_weight):
    attended = lax.map(attend_one, (queries, keys, values, lengths))
    attn_out = jnp.dot(attended, out_weight, preferred_element_type=jnp.float32)
    state = jnp.take(residual, batch_of_slot, axis=0).astype(jnp.float32) + attn_out
    mean_square = lax.optimization_barrier(jnp.sum(state * state, axis=1)) / D
    normed = (state * lax.rsqrt(mean_square + 1e-05)[:, None] * norm_gain).astype(jnp.bfloat16)
    gate = jnp.dot(normed, gate_weight, preferred_element_type=jnp.float32)
    up_proj = jnp.dot(normed, up_weight, preferred_element_type=jnp.float32)
    hidden = (jax.nn.silu(gate) * up_proj).astype(jnp.bfloat16)
    ffn_out = jnp.dot(hidden, down_weight, preferred_element_type=jnp.float32)
    return (state + ffn_out).astype(jnp.bfloat16)
```

```python
import functools

import jax
import jax.numpy as jnp
from jax import lax
from jax.experimental import pallas as pl
from jax.experimental.pallas import tpu as pltpu
from jax.sharding import PartitionSpec as P

QUERY_HEADS = 64
KEY_VALUE_HEADS = 8
HEAD_WIDTH = 128
EPSILON = 1e-05
MESH = pl.DeviceIdType.MESH
BF16 = jnp.bfloat16
F32 = jnp.float32
LAG_SUM, LAG_HIDDEN, LAG_FORWARD, LAG_DOWN = 1, 3, 5, 6
OWN_RING = 4


def attend(queries, keys, values, lengths):
    request_list = queries.shape[0]
    every_position = keys.shape[1]
    group_width = QUERY_HEADS // KEY_VALUE_HEADS
    query_table = queries.reshape(request_list, KEY_VALUE_HEADS, group_width, HEAD_WIDTH)
    key_table = keys.reshape(request_list, every_position, KEY_VALUE_HEADS, HEAD_WIDTH)
    value_table = values.reshape(request_list, every_position, KEY_VALUE_HEADS, HEAD_WIDTH)
    scores = jnp.einsum(
        "rkgd,rpkd->rkgp", query_table, key_table, preferred_element_type=jnp.float32
    ) * HEAD_WIDTH ** (-0.5)
    positions = lax.broadcasted_iota(jnp.int32, scores.shape, 3)
    in_cache = positions < lengths[:, None, None, None]
    scores = jnp.where(in_cache, scores, -jnp.inf)
    row_max = jnp.max(scores, axis=3, keepdims=True)
    weights = jnp.exp(scores - row_max)
    probabilities = (weights / jnp.sum(weights, axis=3, keepdims=True)).astype(jnp.bfloat16)
    attended = jnp.einsum(
        "rkgp,rpkd->rkgd", probabilities, value_table, preferred_element_type=jnp.float32
    )
    return attended.astype(jnp.bfloat16).reshape(request_list, QUERY_HEADS * HEAD_WIDTH)


def pieces(size):
    return size // 512 if size % 512 == 0 else size // 128


def layer_kernel(
    n, s, r,
    att_ref, res_ref, gain_ref, ow_hbm, gw_hbm, uw_hbm, dw_hbm,
    out_ref,
    ow, gw, uw, dw, cols, xin, part32, part16, rs, state, sqs, nf,
    gu32, gsend, grecv, gown, xsend, xrecv, hid, acc, dsend, drecv, fin, outs,
    ow_sem, gw_sem, uw_sem, dw_sem, own_sem,
    a1_send, a2_send, a_recv, rs_send, rs_recv, sq_send, sq_recv, nf_send, nf_recv,
    g_send, g_recv, x_send, x_recv, h_send, h_recv, d_send, d_recv, f_send, f_recv,
):
    X = s // 2
    R = s * r
    C = ow.shape[0]
    W = ow.shape[1]
    K, M, fc = hid.shape
    Q = n * r
    NC = part32.shape[0]
    wc = W // NC
    D = C * n
    t = lax.axis_index("tp")
    j = lax.axis_index("sec")
    x = j // 2
    c = j % 2
    mate = x * 2 + (1 - c)

    def tp_at(d):
        return lax.rem(t + d, n)

    def sec_at(d):
        return lax.rem(j + d, s)

    def x_at(d):
        return lax.rem(x + d, X)

    def remote(src, dst, send, recv, **where):
        return pltpu.make_async_remote_copy(
            src_ref=src, dst_ref=dst, send_sem=send, recv_sem=recv,
            device_id=where, device_id_type=MESH,
        )

    def rows(index, count):
        return pl.ds(pl.multiple_of(index * count, count), count)

    def ow_copy(i):
        at = pl.ds(i * (C // 4), C // 4)
        return pltpu.make_async_copy(ow_hbm.at[at], ow.at[at], ow_sem.at[i])

    def gw_copy(k):
        at = pl.ds(pl.multiple_of(k * fc, fc), fc)
        return pltpu.make_async_copy(gw_hbm.at[:, at], gw.at[k], gw_sem.at[k])

    def uw_copy(k):
        at = pl.ds(pl.multiple_of(k * fc, fc), fc)
        return pltpu.make_async_copy(uw_hbm.at[:, at], uw.at[k], uw_sem.at[k])

    def dw_copy(k):
        return pltpu.make_async_copy(dw_hbm.at[rows(k, fc)], dw.at[k], dw_sem.at[k])

    for i in range(4):
        ow_copy(i).start()

    barrier = pltpu.get_barrier_semaphore()
    for d in range(1, n):
        pl.semaphore_signal(barrier, inc=1, device_id={"tp": tp_at(d)}, device_id_type=MESH)
    for d in range(1, s):
        pl.semaphore_signal(barrier, inc=1, device_id={"sec": sec_at(d)}, device_id_type=MESH)
    pl.semaphore_wait(barrier, n + s - 2)

    def feature(tt):
        return att_ref.at[:, pl.ds(pl.multiple_of(tt * C, C), C)]

    def a1(d):
        return remote(feature(tp_at(d)), cols.at[t, j], a1_send.at[d - 1], a_recv.at[t, j], tp=tp_at(d))

    def a1_arrive(tt):
        return remote(cols.at[tt, j], cols.at[tt, j], a1_send.at[0], a_recv.at[tt, j], tp=tp_at(1))

    def a2_block(tt, jj, own=False):
        return feature(t) if own else cols.at[tt, jj]

    def a2_mate(tt, jj, own=False):
        return remote(a2_block(tt, jj, own), cols.at[tt, jj], a2_send.at[tt, jj], a_recv.at[tt, jj], sec=mate)

    def a2_x(tt, d, own=False):
        return remote(
            a2_block(tt, j, own), cols.at[tt, j], a2_send.at[tt, s - 1 + d],
            a_recv.at[tt, j], sec=x_at(d) * 2 + c,
        )

    for d in range(1, n):
        a1(d).start()
    own_copy = pltpu.make_async_copy(feature(t), cols.at[t, j], own_sem)
    own_copy.start()
    for d in range(1, X):
        a2_x(t, d, True).start()
    a2_mate(t, j, True).start()
    for k in range(K):
        gw_copy(k).start()
        uw_copy(k).start()
    for k in range(K):
        dw_copy(k).start()
    for d in range(1, n):
        tt = tp_at(d)
        a1_arrive(tt).wait_recv()
        for e in range(1, X):
            a2_x(tt, e).start()
        a2_mate(tt, j).start()
    for d in range(n):
        tt = tp_at(d)
        for e in range(1, X):
            jj = x_at(e) * 2 + c
            a2_mate(tt, jj).wait_recv()
            a2_mate(tt, jj).start()
    own_copy.wait()
    for d in range(n):
        tt = tp_at(d)
        for e in range(X):
            a2_mate(tt, x_at(e) * 2 + (1 - c)).wait_recv()
    for tt in range(n):
        xin[tt * R:(tt + 1) * R, :] = cols[tt].astype(F32).reshape(R, C).astype(BF16)

    def rs_copy(i, d):
        return remote(
            part16.at[i, rows(tp_at(d), R)], rs.at[i, d - 1],
            rs_send.at[i, d - 1], rs_recv.at[i, d - 1], tp=tp_at(d),
        )

    for i in range(4):
        ow_copy(i).wait()

    @pl.loop(0, NC)
    def _(i):
        at = pl.ds(pl.multiple_of(i * wc, wc), wc)
        product = jnp.dot(xin[...], ow[:, at], preferred_element_type=F32)
        part32[i] = product
        part16[i] = product.astype(BF16)
        for d in range(1, n):
            rs_copy(i, d).start()

    for i in range(NC):
        at = slice(i * wc, (i + 1) * wc)
        total = part32[i, rows(t, R)]
        for d in range(1, n):
            rs_copy(i, d).wait_recv()
            total += rs[i, d - 1].astype(F32)
        state[:, at] = res_ref[:, at].astype(F32) + total

    def sq_copy(d):
        return remote(sqs.at[j], sqs.at[j], sq_send.at[d - 1], sq_recv.at[j], sec=sec_at(d))

    def sq_arrive(jj):
        return remote(sqs.at[jj], sqs.at[jj], sq_send.at[0], sq_recv.at[jj], sec=sec_at(1))

    squares = jnp.sum(state[...] * state[...], axis=1, keepdims=True)
    sqs[j] = jnp.broadcast_to(squares, (R, 128))
    for d in range(1, s):
        sq_copy(d).start()
    for d in range(1, s):
        sq_arrive(sec_at(d)).wait_recv()
    total = sqs[0]
    for jj in range(1, s):
        total += sqs[jj]
    scale = lax.rsqrt(total[:, :1] / (W * s) + EPSILON)
    nf[rows(t, R)] = (state[...] * scale * gain_ref[...]).astype(BF16)

    def nf_copy(d):
        return remote(
            nf.at[rows(t, R)], nf.at[rows(t, R)], nf_send.at[d - 1], nf_recv.at[t], tp=tp_at(d)
        )

    def nf_arrive(tt):
        return remote(
            nf.at[rows(tt, R)], nf.at[rows(tt, R)], nf_send.at[0], nf_recv.at[tt], tp=tp_at(1)
        )

    for d in range(1, n):
        nf_copy(d).start()
    acc[...] = jnp.zeros_like(acc)
    for d in range(1, n):
        nf_arrive(tp_at(d)).wait_recv()

    def g_copy(k):
        return remote(gsend.at[k], grecv.at[k], g_send.at[k], g_recv.at[k], sec=mate)

    def x_copy(k, d):
        return remote(
            xsend.at[k, d - 1], xrecv.at[k, d - 1], x_send.at[k, d - 1], x_recv.at[k, d - 1],
            sec=x_at(d) * 2 + c,
        )

    def h_mate(k, jj):
        at = hid.at[k, rows(jj, Q)]
        return remote(at, at, h_send.at[k, jj], h_recv.at[k, jj], sec=mate)

    def h_x(k, d):
        at = hid.at[k, rows(j, Q)]
        return remote(at, at, h_send.at[k, s - 1 + d], h_recv.at[k, j], sec=x_at(d) * 2 + c)

    @pl.loop(0, K + LAG_DOWN)
    def _(step):
        @pl.when(step < K)
        def _():
            k = step
            slot = lax.rem(k, 2)
            gw_copy(k).wait()
            uw_copy(k).wait()
            gu32[slot, :, :fc] = jnp.dot(nf[...], gw[k], preferred_element_type=F32)
            gu32[slot, :, fc:] = jnp.dot(nf[...], uw[k], preferred_element_type=F32)
            for xx in range(X):
                gsend[k, xx] = gu32[slot, rows(2 * xx + 1 - c, Q)].astype(BF16)
            g_copy(k).start()

        @pl.when((step >= LAG_SUM) & (step < K + LAG_SUM))
        def _():
            k = step - LAG_SUM
            slot = lax.rem(k, 2)
            g_copy(k).wait_recv()
            for d in range(1, X):
                xx = x_at(d)
                both = gu32[slot, rows(2 * xx + c, Q)] + grecv[k, xx].astype(F32)
                xsend[k, d - 1] = both.astype(BF16)
                x_copy(k, d).start()
            gown[lax.rem(k, OWN_RING)] = gu32[slot, rows(j, Q)] + grecv[k, x].astype(F32)

        @pl.when((step >= LAG_HIDDEN) & (step < K + LAG_HIDDEN))
        def _():
            k = step - LAG_HIDDEN
            both = gown[lax.rem(k, OWN_RING)]
            for d in range(1, X):
                x_copy(k, d).wait_recv()
                both += xrecv[k, d - 1].astype(F32)
            gate = both[:, :fc]
            hid[k, rows(j, Q)] = (gate / (1.0 + jnp.exp(-gate)) * both[:, fc:]).astype(BF16)
            for d in range(1, X):
                h_x(k, d).start()
            h_mate(k, j).start()

        @pl.when((step >= LAG_FORWARD) & (step < K + LAG_FORWARD))
        def _():
            k = step - LAG_FORWARD
            for d in range(1, X):
                jj = x_at(d) * 2 + c
                h_mate(k, jj).wait_recv()
                h_mate(k, jj).start()

        @pl.when(step >= LAG_DOWN)
        def _():
            k = step - LAG_DOWN
            dw_copy(k).wait()
            for d in range(X):
                h_mate(k, x_at(d) * 2 + (1 - c)).wait_recv()
            acc[...] += jnp.dot(hid[k], dw[k], preferred_element_type=F32)

    def d_copy(d):
        return remote(
            dsend.at[rows(tp_at(d), R)], drecv.at[d - 1], d_send.at[d - 1], d_recv.at[d - 1],
            tp=tp_at(d),
        )

    dsend[...] = acc[...].astype(BF16)
    for d in range(1, n):
        d_copy(d).start()
    final = state[...] + acc[rows(t, R)]
    for d in range(1, n):
        d_copy(d).wait_recv()
        final += drecv[d - 1].astype(F32)
    fin[...] = final.reshape(s, r, W).astype(BF16)

    def f_copy(d):
        return remote(
            fin.at[sec_at(d)], outs.at[j], f_send.at[d - 1], f_recv.at[j], sec=sec_at(d)
        )

    def f_arrive(jj):
        return remote(fin.at[jj], outs.at[jj], f_send.at[0], f_recv.at[jj], sec=sec_at(1))

    for d in range(1, s):
        f_copy(d).start()
    outs[j] = fin[j]
    for d in range(1, s):
        f_arrive(sec_at(d)).wait_recv()
    for jj in range(s):
        out_ref[:, jj * W:(jj + 1) * W] = outs[jj]

    for d in range(1, n):
        a1(d).wait_send()
        nf_copy(d).wait_send()
        d_copy(d).wait_send()
    for d in range(1, s):
        sq_copy(d).wait_send()
        f_copy(d).wait_send()
    for d in range(n):
        tt = tp_at(d)
        for e in range(1, X):
            a2_x(tt, e, d == 0).wait_send()
            a2_mate(tt, x_at(e) * 2 + c).wait_send()
        a2_mate(tt, j, d == 0).wait_send()
    for i in range(NC):
        for d in range(1, n):
            rs_copy(i, d).wait_send()

    @pl.loop(0, K)
    def _(k):
        g_copy(k).wait_send()
        for d in range(1, X):
            x_copy(k, d).wait_send()
            h_x(k, d).wait_send()
            h_mate(k, x_at(d) * 2 + c).wait_send()
        h_mate(k, j).wait_send()


def layer(n, s, attended, rest, gain, out_weight, gate_weight, up_weight, down_weight):
    r, D = attended.shape
    X = s // 2
    R = s * r
    M = n * R
    Q = n * r
    C, W = out_weight.shape
    F = gate_weight.shape[1]
    K = pieces(F)
    fc = F // K
    NC = pieces(W)
    wc = W // NC
    XP = max(X - 1, 1)
    dma = pltpu.SemaphoreType.DMA
    vmem = pl.BlockSpec(memory_space=pltpu.VMEM)
    hbm = pl.BlockSpec(memory_space=pl.ANY)
    return pl.pallas_call(
        functools.partial(layer_kernel, n, s, r),
        out_shape=jax.ShapeDtypeStruct((r, D), BF16),
        in_specs=[vmem] * 3 + [hbm] * 4,
        out_specs=vmem,
        scratch_shapes=[
            pltpu.VMEM((C, W), BF16),
            pltpu.VMEM((K, W, fc), BF16),
            pltpu.VMEM((K, W, fc), BF16),
            pltpu.VMEM((K, fc, W), BF16),
            pltpu.VMEM((n, s, r, C), BF16),
            pltpu.VMEM((M, C), BF16),
            pltpu.VMEM((NC, M, wc), F32),
            pltpu.VMEM((NC, M, wc), BF16),
            pltpu.VMEM((NC, n - 1, R, wc), BF16),
            pltpu.VMEM((R, W), F32),
            pltpu.VMEM((s, R, 128), F32),
            pltpu.VMEM((M, W), BF16),
            pltpu.VMEM((2, M, 2 * fc), F32),
            pltpu.VMEM((K, X, Q, 2 * fc), BF16),
            pltpu.VMEM((K, X, Q, 2 * fc), BF16),
            pltpu.VMEM((OWN_RING, Q, 2 * fc), F32),
            pltpu.VMEM((K, XP, Q, 2 * fc), BF16),
            pltpu.VMEM((K, XP, Q, 2 * fc), BF16),
            pltpu.VMEM((K, M, fc), BF16),
            pltpu.VMEM((M, W), F32),
            pltpu.VMEM((M, W), BF16),
            pltpu.VMEM((n - 1, R, W), BF16),
            pltpu.VMEM((s, r, W), BF16),
            pltpu.VMEM((s, r, W), BF16),
            dma((4,)), dma((K,)), dma((K,)), dma((K,)), dma,
            dma((n - 1,)), dma((n, s + XP)), dma((n, s)),
            dma((NC, n - 1)), dma((NC, n - 1)),
            dma((s - 1,)), dma((s,)),
            dma((n - 1,)), dma((n,)),
            dma((K,)), dma((K,)),
            dma((K, XP)), dma((K, XP)),
            dma((K, s + XP)), dma((K, s)),
            dma((n - 1,)), dma((n - 1,)),
            dma((s - 1,)), dma((s,)),
        ],
        compiler_params=pltpu.CompilerParams(
            collective_id=0, has_side_effects=True, vmem_limit_bytes=67043328
        ),
        name="layer",
    )(attended, rest, gain, out_weight, gate_weight, up_weight, down_weight)


def local(
    queries,
    keys,
    values,
    lengths,
    batch_of_slot,
    residual,
    out_weight,
    norm_gain,
    gate_weight,
    up_weight,
    down_weight,
):
    r = queries.shape[0]
    n = lax.axis_size("tp")
    s = lax.axis_size("sec")
    t = lax.axis_index("tp")
    attended = attend(queries, keys, values, lengths)
    slots = batch_of_slot.reshape(s, n, r)
    own_slots = lax.dynamic_index_in_dim(slots, t, 1, keepdims=False).reshape(s * r)
    rest = jnp.take(residual, own_slots, axis=0)
    return layer(
        n, s, attended, rest, norm_gain.reshape(1, -1),
        out_weight, gate_weight, up_weight, down_weight,
    )


def solution(mesh):
    return jax.shard_map(
        local,
        mesh=mesh,
        in_specs=(
            P(("parts", "sec", "tp"), None),
            P(("parts", "sec", "tp"), None, None),
            P(("parts", "sec", "tp"), None, None),
            P(("parts", "sec", "tp")),
            P("parts"),
            P("parts", "sec"),
            P("tp", "sec"),
            P("sec"),
            P("sec", "tp"),
            P("sec", "tp"),
            P("tp", "sec"),
        ),
        out_specs=P(("parts", "sec", "tp"), None),
        check_vma=False,
    )
```

```python
import functools

import jax
import jax.numpy as jnp
from jax import lax
from jax.experimental import pallas as pl
from jax.experimental.pallas import tpu as pltpu
from jax.sharding import PartitionSpec as P

QUERY_HEADS = 64
KEY_VALUE_HEADS = 8
HEAD_WIDTH = 128
EPSILON = 1e-05
MESH = pl.DeviceIdType.MESH
BF16 = jnp.bfloat16
F32 = jnp.float32
LAG_SUM, LAG_HIDDEN, LAG_FORWARD, LAG_DOWN = 1, 3, 5, 6
OWN_RING = 4


def pieces(size):
    return size // 512 if size % 512 == 0 else size // 128


def layer_kernel(
    n, s, r,
    query_ref, length_ref, slot_ref, gain_ref, key_hbm, value_hbm, res_hbm, ow_hbm, gw_hbm, uw_hbm, dw_hbm,
    out_ref,
    ow, gw, uw, dw, att_ref, q32, o32, cols, xin, part32, part16, rs, state, sqs, nf,
    gu32, gsend, grecv, gown, xsend, xrecv, hid, acc, dsend, drecv, fin, outs, cache,
    kv_sem, res_sem, ow_sem, gw_sem, uw_sem, dw_sem, own_sem,
    a1_send, a2_send, a_recv, rs_send, rs_recv, sq_send, sq_recv, nf_send, nf_recv,
    g_send, g_recv, x_send, x_recv, h_send, h_recv, d_send, d_recv, f_send, f_recv,
):
    X = s // 2
    R = s * r
    C = ow.shape[0]
    W = ow.shape[1]
    K, M, fc = hid.shape
    Q = n * r
    NC = part32.shape[0]
    wc = W // NC
    D = C * n
    t = lax.axis_index("tp")
    j = lax.axis_index("sec")
    x = j // 2
    c = j % 2
    mate = x * 2 + (1 - c)

    def tp_at(d):
        return lax.rem(t + d, n)

    def sec_at(d):
        return lax.rem(j + d, s)

    def x_at(d):
        return lax.rem(x + d, X)

    def remote(src, dst, send, recv, **where):
        return pltpu.make_async_remote_copy(
            src_ref=src, dst_ref=dst, send_sem=send, recv_sem=recv,
            device_id=where, device_id_type=MESH,
        )

    def rows(index, count):
        return pl.ds(pl.multiple_of(index * count, count), count)

    def ow_copy(i):
        at = pl.ds(i * (C // 4), C // 4)
        return pltpu.make_async_copy(ow_hbm.at[at], ow.at[at], ow_sem.at[i])

    def gw_copy(k):
        at = pl.ds(pl.multiple_of(k * fc, fc), fc)
        return pltpu.make_async_copy(gw_hbm.at[:, at], gw.at[k], gw_sem.at[k])

    def uw_copy(k):
        at = pl.ds(pl.multiple_of(k * fc, fc), fc)
        return pltpu.make_async_copy(uw_hbm.at[:, at], uw.at[k], uw_sem.at[k])

    def dw_copy(k):
        return pltpu.make_async_copy(dw_hbm.at[rows(k, fc)], dw.at[k], dw_sem.at[k])

    P_, KW = key_hbm.shape[1:]
    G = KEY_VALUE_HEADS // 2
    group_width = QUERY_HEADS // KEY_VALUE_HEADS
    heads = 2 * group_width
    per = n // G
    first = t * G // n

    def group(i):
        return lax.rem(first + 1 + i, G)

    def columns(g):
        return pl.ds(pl.multiple_of(g * 2 * HEAD_WIDTH, 2 * HEAD_WIDTH), 2 * HEAD_WIDTH)

    def block(b, g):
        if cache.shape[0] > 1:
            return cache.at[b, :, columns(g)]
        high, wide = fc // P_, W // KW
        spot, rest = b // (high * wide), b % (high * wide)
        offset = (rest % wide) * KW
        at = pl.ds(pl.multiple_of(offset + g * 2 * HEAD_WIDTH, 2 * HEAD_WIDTH), 2 * HEAD_WIDTH)
        return dw.at[spot, pl.ds((rest // wide) * P_, P_), at]

    def key_copy(i, g):
        return pltpu.make_async_copy(key_hbm.at[i, :, columns(g)], block(i, g), kv_sem.at[g, i])

    def value_copy(i, g):
        return pltpu.make_async_copy(
            value_hbm.at[i, :, columns(g)], block(r + i, g), kv_sem.at[g, r + i]
        )

    @pl.loop(0, G)
    def _(step):
        g = group(step)
        for i in range(r):
            key_copy(i, g).start()
            value_copy(i, g).start()

    res_copy = pltpu.make_async_copy(res_hbm, dsend, res_sem)
    res_copy.start()
    for i in range(4):
        ow_copy(i).start()

    barrier = pltpu.get_barrier_semaphore()
    for d in range(1, n):
        pl.semaphore_signal(barrier, inc=1, device_id={"tp": tp_at(d)}, device_id_type=MESH)
    for d in range(1, s):
        pl.semaphore_signal(barrier, inc=1, device_id={"sec": sec_at(d)}, device_id_type=MESH)
    for h in range(QUERY_HEADS):
        at = slice(h * HEAD_WIDTH, (h + 1) * HEAD_WIDTH)
        q32[:, h, :] = query_ref[:, at].astype(F32)
    for k in range(K):
        gw_copy(k).start()
        uw_copy(k).start()
    pl.semaphore_wait(barrier, n + s - 2)

    def feature(tt):
        return att_ref.at[:, pl.ds(pl.multiple_of(tt * C, C), C)]

    def a1(tt):
        return remote(feature(tt), cols.at[t, j], a1_send.at[tt], a_recv.at[t, j], tp=tt)

    def a1_arrive(tt):
        return remote(cols.at[tt, j], cols.at[tt, j], a1_send.at[0], a_recv.at[tt, j], tp=tp_at(1))

    def a2_block(tt, jj, own=False):
        return feature(t) if own else cols.at[tt, jj]

    def a2_mate(tt, jj, own=False):
        return remote(a2_block(tt, jj, own), cols.at[tt, jj], a2_send.at[tt, jj], a_recv.at[tt, jj], sec=mate)

    def a2_x(tt, d, own=False):
        return remote(
            a2_block(tt, j, own), cols.at[tt, j], a2_send.at[tt, s - 1 + d],
            a_recv.at[tt, j], sec=x_at(d) * 2 + c,
        )

    @pl.loop(0, G)
    def _(step):
        g = group(step)
        upper = lax.broadcasted_iota(jnp.int32, (heads, HEAD_WIDTH), 0) < group_width
        positions = lax.broadcasted_iota(jnp.int32, (heads, P_), 1)
        for i in range(r):
            key_copy(i, g).wait()
            value_copy(i, g).wait()
        for i in range(r):
            query = q32[i, rows(g, heads)]
            query = jnp.concatenate(
                [jnp.where(upper, query, 0.0), jnp.where(upper, 0.0, query)], axis=1
            ).astype(BF16)
            scores = lax.dot_general(
                query, block(i, g)[...], (((1,), (1,)), ((), ())), preferred_element_type=F32
            ) * HEAD_WIDTH ** (-0.5)
            scores = jnp.where(positions < length_ref[i], scores, -jnp.inf)
            weights = jnp.exp(scores - jnp.max(scores, axis=1, keepdims=True))
            probs = (weights / jnp.sum(weights, axis=1, keepdims=True)).astype(BF16)
            both = jnp.dot(probs, block(r + i, g)[...], preferred_element_type=F32)
            o32[i] = jnp.where(upper, both[:, :HEAD_WIDTH], both[:, HEAD_WIDTH:])
        for h in range(heads):
            at = pl.ds(pl.multiple_of((g * heads + h) * HEAD_WIDTH, HEAD_WIDTH), HEAD_WIDTH)
            att_ref[:, at] = o32[:, h, :].astype(BF16)
        for e in range(per):
            tt = g * per + e

            @pl.when(tt != t)
            def _():
                a1(tt).start()

    own_copy = pltpu.make_async_copy(feature(t), cols.at[t, j], own_sem)
    own_copy.start()
    for d in range(1, X):
        a2_x(t, d, True).start()
    a2_mate(t, j, True).start()
    for k in range(K):
        dw_copy(k).start()
    for d in range(1, n):
        tt = tp_at(d)
        a1_arrive(tt).wait_recv()
        for e in range(1, X):
            a2_x(tt, e).start()
        a2_mate(tt, j).start()
    for d in range(n):
        tt = tp_at(d)
        for e in range(1, X):
            jj = x_at(e) * 2 + c
            a2_mate(tt, jj).wait_recv()
            a2_mate(tt, jj).start()
    own_copy.wait()
    for d in range(n):
        tt = tp_at(d)
        for e in range(X):
            a2_mate(tt, x_at(e) * 2 + (1 - c)).wait_recv()
    for tt in range(n):
        xin[tt * R:(tt + 1) * R, :] = cols[tt].astype(F32).reshape(R, C).astype(BF16)

    def rs_copy(i, d):
        return remote(
            part16.at[i, rows(tp_at(d), R)], rs.at[i, d - 1],
            rs_send.at[i, d - 1], rs_recv.at[i, d - 1], tp=tp_at(d),
        )

    for i in range(4):
        ow_copy(i).wait()

    @pl.loop(0, NC)
    def _(i):
        at = pl.ds(pl.multiple_of(i * wc, wc), wc)
        product = jnp.dot(xin[...], ow[:, at], preferred_element_type=F32)
        part32[i] = product
        part16[i] = product.astype(BF16)
        for d in range(1, n):
            rs_copy(i, d).start()

    slot = (
        lax.broadcasted_iota(jnp.int32, (s, r, M), 0) * (n * r) + t * r
        + lax.broadcasted_iota(jnp.int32, (s, r, M), 1)
    )
    mine = jnp.where(lax.broadcasted_iota(jnp.int32, (s, r, M), 2) == slot, 1.0, 0.0)
    batch = lax.broadcasted_iota(jnp.int32, (M, M), 0)
    held = jnp.where(batch == slot_ref[...], 1.0, 0.0).astype(BF16)
    pick = lax.dot_general(
        mine.reshape(R, M).astype(BF16), held, (((1,), (1,)), ((), ())),
        preferred_element_type=F32,
    ).astype(BF16)
    res_copy.wait()
    state[...] = jnp.dot(pick, dsend[...], preferred_element_type=F32)
    for i in range(NC):
        at = slice(i * wc, (i + 1) * wc)
        total = part32[i, rows(t, R)]
        for d in range(1, n):
            rs_copy(i, d).wait_recv()
            total += rs[i, d - 1].astype(F32)
        state[:, at] = state[:, at] + total

    def sq_copy(d):
        return remote(sqs.at[j], sqs.at[j], sq_send.at[d - 1], sq_recv.at[j], sec=sec_at(d))

    def sq_arrive(jj):
        return remote(sqs.at[jj], sqs.at[jj], sq_send.at[0], sq_recv.at[jj], sec=sec_at(1))

    squares = jnp.sum(state[...] * state[...], axis=1, keepdims=True)
    sqs[j] = jnp.broadcast_to(squares, (R, 128))
    for d in range(1, s):
        sq_copy(d).start()
    for d in range(1, s):
        sq_arrive(sec_at(d)).wait_recv()
    total = sqs[0]
    for jj in range(1, s):
        total += sqs[jj]
    scale = lax.rsqrt(total[:, :1] / (W * s) + EPSILON)
    nf[rows(t, R)] = (state[...] * scale * gain_ref[...]).astype(BF16)

    def nf_copy(d):
        return remote(
            nf.at[rows(t, R)], nf.at[rows(t, R)], nf_send.at[d - 1], nf_recv.at[t], tp=tp_at(d)
        )

    def nf_arrive(tt):
        return remote(
            nf.at[rows(tt, R)], nf.at[rows(tt, R)], nf_send.at[0], nf_recv.at[tt], tp=tp_at(1)
        )

    for d in range(1, n):
        nf_copy(d).start()
    acc[...] = jnp.zeros_like(acc)
    for d in range(1, n):
        nf_arrive(tp_at(d)).wait_recv()

    def g_copy(k):
        return remote(gsend.at[k], grecv.at[k], g_send.at[k], g_recv.at[k], sec=mate)

    def x_copy(k, d):
        return remote(
            xsend.at[k, d - 1], xrecv.at[k, d - 1], x_send.at[k, d - 1], x_recv.at[k, d - 1],
            sec=x_at(d) * 2 + c,
        )

    def h_mate(k, jj):
        at = hid.at[k, rows(jj, Q)]
        return remote(at, at, h_send.at[k, jj], h_recv.at[k, jj], sec=mate)

    def h_x(k, d):
        at = hid.at[k, rows(j, Q)]
        return remote(at, at, h_send.at[k, s - 1 + d], h_recv.at[k, j], sec=x_at(d) * 2 + c)

    @pl.loop(0, K + LAG_DOWN)
    def _(step):
        @pl.when(step < K)
        def _():
            k = step
            slot = lax.rem(k, 2)
            gw_copy(k).wait()
            uw_copy(k).wait()
            gu32[slot, :, :fc] = jnp.dot(nf[...], gw[k], preferred_element_type=F32)
            gu32[slot, :, fc:] = jnp.dot(nf[...], uw[k], preferred_element_type=F32)
            for xx in range(X):
                gsend[k, xx] = gu32[slot, rows(2 * xx + 1 - c, Q)].astype(BF16)
            g_copy(k).start()

        @pl.when((step >= LAG_SUM) & (step < K + LAG_SUM))
        def _():
            k = step - LAG_SUM
            slot = lax.rem(k, 2)
            g_copy(k).wait_recv()
            for d in range(1, X):
                xx = x_at(d)
                both = gu32[slot, rows(2 * xx + c, Q)] + grecv[k, xx].astype(F32)
                xsend[k, d - 1] = both.astype(BF16)
                x_copy(k, d).start()
            gown[lax.rem(k, OWN_RING)] = gu32[slot, rows(j, Q)] + grecv[k, x].astype(F32)

        @pl.when((step >= LAG_HIDDEN) & (step < K + LAG_HIDDEN))
        def _():
            k = step - LAG_HIDDEN
            both = gown[lax.rem(k, OWN_RING)]
            for d in range(1, X):
                x_copy(k, d).wait_recv()
                both += xrecv[k, d - 1].astype(F32)
            gate = both[:, :fc]
            hid[k, rows(j, Q)] = (gate / (1.0 + jnp.exp(-gate)) * both[:, fc:]).astype(BF16)
            for d in range(1, X):
                h_x(k, d).start()
            h_mate(k, j).start()

        @pl.when((step >= LAG_FORWARD) & (step < K + LAG_FORWARD))
        def _():
            k = step - LAG_FORWARD
            for d in range(1, X):
                jj = x_at(d) * 2 + c
                h_mate(k, jj).wait_recv()
                h_mate(k, jj).start()

        @pl.when(step >= LAG_DOWN)
        def _():
            k = step - LAG_DOWN
            dw_copy(k).wait()
            for d in range(X):
                h_mate(k, x_at(d) * 2 + (1 - c)).wait_recv()
            acc[...] += jnp.dot(hid[k], dw[k], preferred_element_type=F32)

    def d_copy(d):
        return remote(
            dsend.at[rows(tp_at(d), R)], drecv.at[d - 1], d_send.at[d - 1], d_recv.at[d - 1],
            tp=tp_at(d),
        )

    dsend[...] = acc[...].astype(BF16)
    for d in range(1, n):
        d_copy(d).start()
    final = state[...] + acc[rows(t, R)]
    for d in range(1, n):
        d_copy(d).wait_recv()
        final += drecv[d - 1].astype(F32)
    fin[...] = final.reshape(s, r, W).astype(BF16)

    def f_copy(d):
        return remote(
            fin.at[sec_at(d)], outs.at[j], f_send.at[d - 1], f_recv.at[j], sec=sec_at(d)
        )

    def f_arrive(jj):
        return remote(fin.at[jj], outs.at[jj], f_send.at[0], f_recv.at[jj], sec=sec_at(1))

    for d in range(1, s):
        f_copy(d).start()
    outs[j] = fin[j]
    for d in range(1, s):
        f_arrive(sec_at(d)).wait_recv()
    for jj in range(s):
        out_ref[:, jj * W:(jj + 1) * W] = outs[jj]

    for d in range(1, n):
        a1(tp_at(d)).wait_send()
        nf_copy(d).wait_send()
        d_copy(d).wait_send()
    for d in range(1, s):
        sq_copy(d).wait_send()
        f_copy(d).wait_send()
    for d in range(n):
        tt = tp_at(d)
        for e in range(1, X):
            a2_x(tt, e, d == 0).wait_send()
            a2_mate(tt, x_at(e) * 2 + c).wait_send()
        a2_mate(tt, j, d == 0).wait_send()
    for i in range(NC):
        for d in range(1, n):
            rs_copy(i, d).wait_send()

    @pl.loop(0, K)
    def _(k):
        g_copy(k).wait_send()
        for d in range(1, X):
            x_copy(k, d).wait_send()
            h_x(k, d).wait_send()
            h_mate(k, x_at(d) * 2 + c).wait_send()
        h_mate(k, j).wait_send()


def layer(n, s, queries, lengths, slots, gain, keys, values, residual, out_weight, gate_weight, up_weight, down_weight):
    r, D = queries.shape
    P_, KW = keys.shape[1:]
    assert n % (KEY_VALUE_HEADS // 2) == 0
    X = s // 2
    R = s * r
    M = n * R
    Q = n * r
    C, W = out_weight.shape
    F = gate_weight.shape[1]
    K = pieces(F)
    fc = F // K
    NC = pieces(W)
    wc = W // NC
    XP = max(X - 1, 1)
    inside = fc % P_ == 0 and W % KW == 0 and K * (fc // P_) * (W // KW) >= 2 * r
    cache = (1, 16, 128) if inside else (2 * r, P_, KW)
    dma = pltpu.SemaphoreType.DMA
    vmem = pl.BlockSpec(memory_space=pltpu.VMEM)
    hbm = pl.BlockSpec(memory_space=pl.ANY)
    return pl.pallas_call(
        functools.partial(layer_kernel, n, s, r),
        out_shape=jax.ShapeDtypeStruct((r, D), BF16),
        in_specs=[vmem, pl.BlockSpec(memory_space=pltpu.SMEM), vmem, vmem] + [hbm] * 7,
        out_specs=vmem,
        scratch_shapes=[
            pltpu.VMEM((C, W), BF16),
            pltpu.VMEM((K, W, fc), BF16),
            pltpu.VMEM((K, W, fc), BF16),
            pltpu.VMEM((K, fc, W), BF16),
            pltpu.VMEM((r, D), BF16),
            pltpu.VMEM((r, QUERY_HEADS, HEAD_WIDTH), F32),
            pltpu.VMEM((r, 2 * QUERY_HEADS // KEY_VALUE_HEADS, HEAD_WIDTH), F32),
            pltpu.VMEM((n, s, r, C), BF16),
            pltpu.VMEM((M, C), BF16),
            pltpu.VMEM((NC, M, wc), F32),
            pltpu.VMEM((NC, M, wc), BF16),
            pltpu.VMEM((NC, n - 1, R, wc), BF16),
            pltpu.VMEM((R, W), F32),
            pltpu.VMEM((s, R, 128), F32),
            pltpu.VMEM((M, W), BF16),
            pltpu.VMEM((2, M, 2 * fc), F32),
            pltpu.VMEM((K, X, Q, 2 * fc), BF16),
            pltpu.VMEM((K, X, Q, 2 * fc), BF16),
            pltpu.VMEM((OWN_RING, Q, 2 * fc), F32),
            pltpu.VMEM((K, XP, Q, 2 * fc), BF16),
            pltpu.VMEM((K, XP, Q, 2 * fc), BF16),
            pltpu.VMEM((K, M, fc), BF16),
            pltpu.VMEM((M, W), F32),
            pltpu.VMEM((M, W), BF16),
            pltpu.VMEM((n - 1, R, W), BF16),
            pltpu.VMEM((s, r, W), BF16),
            pltpu.VMEM((s, r, W), BF16),
            pltpu.VMEM(cache, BF16),
            dma((KEY_VALUE_HEADS // 2, 2 * r)), dma,
            dma((4,)), dma((K,)), dma((K,)), dma((K,)), dma,
            dma((n,)), dma((n, s + XP)), dma((n, s)),
            dma((NC, n - 1)), dma((NC, n - 1)),
            dma((s - 1,)), dma((s,)),
            dma((n - 1,)), dma((n,)),
            dma((K,)), dma((K,)),
            dma((K, XP)), dma((K, XP)),
            dma((K, s + XP)), dma((K, s)),
            dma((n - 1,)), dma((n - 1,)),
            dma((s - 1,)), dma((s,)),
        ],
        compiler_params=pltpu.CompilerParams(
            collective_id=0, has_side_effects=True, vmem_limit_bytes=67043328
        ),
        name="layer",
    )(queries, lengths, slots, gain, keys, values, residual, out_weight, gate_weight, up_weight, down_weight)


def local(
    queries,
    keys,
    values,
    lengths,
    batch_of_slot,
    residual,
    out_weight,
    norm_gain,
    gate_weight,
    up_weight,
    down_weight,
):
    return layer(
        lax.axis_size("tp"), lax.axis_size("sec"), queries, lengths,
        batch_of_slot.reshape(1, -1), norm_gain.reshape(1, -1), keys, values, residual,
        out_weight, gate_weight, up_weight, down_weight,
    )


def solution(mesh):
    return jax.shard_map(
        local,
        mesh=mesh,
        in_specs=(
            P(("parts", "sec", "tp"), None),
            P(("parts", "sec", "tp"), None, None),
            P(("parts", "sec", "tp"), None, None),
            P(("parts", "sec", "tp")),
            P("parts"),
            P("parts", "sec"),
            P("tp", "sec"),
            P("sec"),
            P("sec", "tp"),
            P("sec", "tp"),
            P("tp", "sec"),
        ),
        out_specs=P(("parts", "sec", "tp"), None),
        check_vma=False,
    )
```

```python
import functools

import jax
import jax.numpy as jnp
from jax import lax
from jax.experimental import pallas as pl
from jax.experimental.pallas import tpu as pltpu
from jax.sharding import PartitionSpec as P

QUERY_HEADS = 64
KEY_VALUE_HEADS = 8
HEAD_WIDTH = 128
EPSILON = 1e-05
MESH = pl.DeviceIdType.MESH
BF16 = jnp.bfloat16
F32 = jnp.float32
LAG_SUM, LAG_HIDDEN, LAG_FORWARD, LAG_DOWN = 1, 3, 5, 6
OWN_RING = 4


def pieces(size):
    return size // 512 if size % 512 == 0 else size // 128


def layer_kernel(
    n, s, r,
    query_ref, length_ref, slot_ref, gain_ref, key_hbm, value_hbm, res_hbm, ow_hbm, gw_hbm, uw_hbm, dw_hbm,
    out_ref,
    ow, gw, uw, dw, att_ref, q32, o32, cols, xin, part32, part16, rs, state, sqs, nf,
    gu32, gsend, grecv, gown, xsend, xrecv, hid, acc, dsend, drecv, fin, outs, cache,
    kv_sem, res_sem, ow_sem, gw_sem, uw_sem, dw_sem, own_sem,
    a1_send, a2_send, a_recv, rs_send, rs_recv, sq_send, sq_recv, nf_send, nf_recv,
    g_send, g_recv, x_send, x_recv, h_send, h_recv, d_send, d_recv, f_send, f_recv,
):
    X = s // 2
    R = s * r
    C = ow.shape[0]
    W = ow.shape[1]
    K, M, fc = hid.shape
    Q = n * r
    NC = part32.shape[0]
    wc = W // NC
    D = C * n
    t = lax.axis_index("tp")
    j = lax.axis_index("sec")
    x = j // 2
    c = j % 2
    mate = x * 2 + (1 - c)

    def tp_at(d):
        return lax.rem(t + d, n)

    def sec_at(d):
        return lax.rem(j + d, s)

    def x_at(d):
        return lax.rem(x + d, X)

    def remote(src, dst, send, recv, **where):
        return pltpu.make_async_remote_copy(
            src_ref=src, dst_ref=dst, send_sem=send, recv_sem=recv,
            device_id=where, device_id_type=MESH,
        )

    def rows(index, count):
        return pl.ds(pl.multiple_of(index * count, count), count)

    def ow_copy(i):
        at = pl.ds(i * (C // 4), C // 4)
        return pltpu.make_async_copy(ow_hbm.at[at], ow.at[at], ow_sem.at[i])

    def gw_copy(k):
        at = pl.ds(pl.multiple_of(k * fc, fc), fc)
        return pltpu.make_async_copy(gw_hbm.at[:, at], gw.at[k], gw_sem.at[k])

    def uw_copy(k):
        at = pl.ds(pl.multiple_of(k * fc, fc), fc)
        return pltpu.make_async_copy(uw_hbm.at[:, at], uw.at[k], uw_sem.at[k])

    def dw_copy(k):
        return pltpu.make_async_copy(dw_hbm.at[rows(k, fc)], dw.at[k], dw_sem.at[k])

    P_, KW = key_hbm.shape[1:]
    G = KEY_VALUE_HEADS // 2
    group_width = QUERY_HEADS // KEY_VALUE_HEADS
    heads = 2 * group_width
    per = n // G
    first = t * G // n

    def group(i):
        return lax.rem(first + 1 + i, G)

    def columns(g):
        return pl.ds(pl.multiple_of(g * 2 * HEAD_WIDTH, 2 * HEAD_WIDTH), 2 * HEAD_WIDTH)

    def block(b, g):
        if cache.shape[0] > 1:
            return cache.at[b, :, columns(g)]
        high, wide = fc // P_, W // KW
        spot, rest = b // (high * wide), b % (high * wide)
        offset = (rest % wide) * KW
        at = pl.ds(pl.multiple_of(offset + g * 2 * HEAD_WIDTH, 2 * HEAD_WIDTH), 2 * HEAD_WIDTH)
        return dw.at[spot, pl.ds((rest // wide) * P_, P_), at]

    def key_copy(i, g):
        return pltpu.make_async_copy(key_hbm.at[i, :, columns(g)], block(i, g), kv_sem.at[g, i])

    def value_copy(i, g):
        return pltpu.make_async_copy(
            value_hbm.at[i, :, columns(g)], block(r + i, g), kv_sem.at[g, r + i]
        )

    @pl.loop(0, G)
    def _(step):
        g = group(step)
        for i in range(r):
            key_copy(i, g).start()
            value_copy(i, g).start()

    res_copy = pltpu.make_async_copy(res_hbm, dsend, res_sem)
    res_copy.start()
    for i in range(4):
        ow_copy(i).start()

    barrier = pltpu.get_barrier_semaphore()
    for d in range(1, n):
        pl.semaphore_signal(barrier, inc=1, device_id={"tp": tp_at(d)}, device_id_type=MESH)
    for d in range(1, s):
        pl.semaphore_signal(barrier, inc=1, device_id={"sec": sec_at(d)}, device_id_type=MESH)
    for h in range(QUERY_HEADS):
        at = slice(h * HEAD_WIDTH, (h + 1) * HEAD_WIDTH)
        q32[:, h, :] = query_ref[:, at].astype(F32)
    for k in range(K):
        gw_copy(k).start()
        uw_copy(k).start()
    pl.semaphore_wait(barrier, n + s - 2)

    def feature(tt):
        return att_ref.at[:, pl.ds(pl.multiple_of(tt * C, C), C)]

    def a1(tt):
        return remote(feature(tt), cols.at[t, j], a1_send.at[tt], a_recv.at[t, j], tp=tt)

    def a1_arrive(tt):
        return remote(cols.at[tt, j], cols.at[tt, j], a1_send.at[0], a_recv.at[tt, j], tp=tp_at(1))

    def a2_block(tt, jj, own=False):
        return feature(t) if own else cols.at[tt, jj]

    def a2_mate(tt, jj, own=False):
        return remote(a2_block(tt, jj, own), cols.at[tt, jj], a2_send.at[tt, jj], a_recv.at[tt, jj], sec=mate)

    def a2_x(tt, d, own=False):
        return remote(
            a2_block(tt, j, own), cols.at[tt, j], a2_send.at[tt, s - 1 + d],
            a_recv.at[tt, j], sec=x_at(d) * 2 + c,
        )

    @pl.loop(0, G)
    def _(step):
        g = group(step)
        upper = lax.broadcasted_iota(jnp.int32, (heads, HEAD_WIDTH), 0) < group_width
        positions = lax.broadcasted_iota(jnp.int32, (heads, P_), 1)
        for i in range(r):
            key_copy(i, g).wait()
            value_copy(i, g).wait()
        scores = []
        for i in range(r):
            query = q32[i, rows(g, heads)]
            query = jnp.concatenate(
                [jnp.where(upper, query, 0.0), jnp.where(upper, 0.0, query)], axis=1
            ).astype(BF16)
            one = lax.dot_general(
                query, block(i, g)[...], (((1,), (1,)), ((), ())), preferred_element_type=F32
            ) * HEAD_WIDTH ** (-0.5)
            scores.append(jnp.where(positions < length_ref[i], one, -jnp.inf))
        scores = jnp.concatenate(scores, axis=0)
        weights = jnp.exp(scores - jnp.max(scores, axis=1, keepdims=True))
        probs = (weights / jnp.sum(weights, axis=1, keepdims=True)).astype(BF16)
        for i in range(r):
            both = jnp.dot(
                probs[i * heads:(i + 1) * heads], block(r + i, g)[...], preferred_element_type=F32
            )
            o32[i] = jnp.where(upper, both[:, :HEAD_WIDTH], both[:, HEAD_WIDTH:])
        for h in range(heads):
            at = pl.ds(pl.multiple_of((g * heads + h) * HEAD_WIDTH, HEAD_WIDTH), HEAD_WIDTH)
            att_ref[:, at] = o32[:, h, :].astype(BF16)
        for e in range(per):
            tt = g * per + e

            @pl.when(tt != t)
            def _():
                a1(tt).start()

    own_copy = pltpu.make_async_copy(feature(t), cols.at[t, j], own_sem)
    own_copy.start()
    for d in range(1, X):
        a2_x(t, d, True).start()
    a2_mate(t, j, True).start()
    for k in range(K):
        dw_copy(k).start()
    for d in range(1, n):
        tt = tp_at(d)
        a1_arrive(tt).wait_recv()
        for e in range(1, X):
            a2_x(tt, e).start()
        a2_mate(tt, j).start()
    for d in range(n):
        tt = tp_at(d)
        for e in range(1, X):
            jj = x_at(e) * 2 + c
            a2_mate(tt, jj).wait_recv()
            a2_mate(tt, jj).start()
    own_copy.wait()
    for d in range(n):
        tt = tp_at(d)
        for e in range(X):
            a2_mate(tt, x_at(e) * 2 + (1 - c)).wait_recv()
    for tt in range(n):
        xin[tt * R:(tt + 1) * R, :] = cols[tt].astype(F32).reshape(R, C).astype(BF16)

    def rs_copy(i, d):
        return remote(
            part16.at[i, rows(tp_at(d), R)], rs.at[i, d - 1],
            rs_send.at[i, d - 1], rs_recv.at[i, d - 1], tp=tp_at(d),
        )

    for i in range(4):
        ow_copy(i).wait()

    @pl.loop(0, NC)
    def _(i):
        at = pl.ds(pl.multiple_of(i * wc, wc), wc)
        product = jnp.dot(xin[...], ow[:, at], preferred_element_type=F32)
        part32[i] = product
        part16[i] = product.astype(BF16)
        for d in range(1, n):
            rs_copy(i, d).start()

    slot = (
        lax.broadcasted_iota(jnp.int32, (s, r, M), 0) * (n * r) + t * r
        + lax.broadcasted_iota(jnp.int32, (s, r, M), 1)
    )
    mine = jnp.where(lax.broadcasted_iota(jnp.int32, (s, r, M), 2) == slot, 1.0, 0.0)
    batch = lax.broadcasted_iota(jnp.int32, (M, M), 0)
    held = jnp.where(batch == slot_ref[...], 1.0, 0.0).astype(BF16)
    pick = lax.dot_general(
        mine.reshape(R, M).astype(BF16), held, (((1,), (1,)), ((), ())),
        preferred_element_type=F32,
    ).astype(BF16)
    res_copy.wait()
    state[...] = jnp.dot(pick, dsend[...], preferred_element_type=F32)
    for i in range(NC):
        at = slice(i * wc, (i + 1) * wc)
        total = part32[i, rows(t, R)]
        for d in range(1, n):
            rs_copy(i, d).wait_recv()
            total += rs[i, d - 1].astype(F32)
        state[:, at] = state[:, at] + total

    def sq_copy(d):
        return remote(sqs.at[j], sqs.at[j], sq_send.at[d - 1], sq_recv.at[j], sec=sec_at(d))

    def sq_arrive(jj):
        return remote(sqs.at[jj], sqs.at[jj], sq_send.at[0], sq_recv.at[jj], sec=sec_at(1))

    squares = jnp.sum(state[...] * state[...], axis=1, keepdims=True)
    sqs[j] = jnp.broadcast_to(squares, (R, 128))
    for d in range(1, s):
        sq_copy(d).start()
    for d in range(1, s):
        sq_arrive(sec_at(d)).wait_recv()
    total = sqs[0]
    for jj in range(1, s):
        total += sqs[jj]
    scale = lax.rsqrt(total[:, :1] / (W * s) + EPSILON)
    nf[rows(t, R)] = (state[...] * scale * gain_ref[...]).astype(BF16)

    def nf_copy(d):
        return remote(
            nf.at[rows(t, R)], nf.at[rows(t, R)], nf_send.at[d - 1], nf_recv.at[t], tp=tp_at(d)
        )

    def nf_arrive(tt):
        return remote(
            nf.at[rows(tt, R)], nf.at[rows(tt, R)], nf_send.at[0], nf_recv.at[tt], tp=tp_at(1)
        )

    for d in range(1, n):
        nf_copy(d).start()
    acc[...] = jnp.zeros_like(acc)
    for d in range(1, n):
        nf_arrive(tp_at(d)).wait_recv()

    def g_copy(k):
        return remote(gsend.at[k], grecv.at[k], g_send.at[k], g_recv.at[k], sec=mate)

    def x_copy(k, d):
        return remote(
            xsend.at[k, d - 1], xrecv.at[k, d - 1], x_send.at[k, d - 1], x_recv.at[k, d - 1],
            sec=x_at(d) * 2 + c,
        )

    def h_mate(k, jj):
        at = hid.at[k, rows(jj, Q)]
        return remote(at, at, h_send.at[k, jj], h_recv.at[k, jj], sec=mate)

    def h_x(k, d):
        at = hid.at[k, rows(j, Q)]
        return remote(at, at, h_send.at[k, s - 1 + d], h_recv.at[k, j], sec=x_at(d) * 2 + c)

    @pl.loop(0, K + LAG_DOWN)
    def _(step):
        @pl.when(step < K)
        def _():
            k = step
            slot = lax.rem(k, 2)
            gw_copy(k).wait()
            uw_copy(k).wait()
            gu32[slot, :, :fc] = jnp.dot(nf[...], gw[k], preferred_element_type=F32)
            gu32[slot, :, fc:] = jnp.dot(nf[...], uw[k], preferred_element_type=F32)
            for xx in range(X):
                gsend[k, xx] = gu32[slot, rows(2 * xx + 1 - c, Q)].astype(BF16)
            g_copy(k).start()

        @pl.when((step >= LAG_SUM) & (step < K + LAG_SUM))
        def _():
            k = step - LAG_SUM
            slot = lax.rem(k, 2)
            g_copy(k).wait_recv()
            for d in range(1, X):
                xx = x_at(d)
                both = gu32[slot, rows(2 * xx + c, Q)] + grecv[k, xx].astype(F32)
                xsend[k, d - 1] = both.astype(BF16)
                x_copy(k, d).start()
            gown[lax.rem(k, OWN_RING)] = gu32[slot, rows(j, Q)] + grecv[k, x].astype(F32)

        @pl.when((step >= LAG_HIDDEN) & (step < K + LAG_HIDDEN))
        def _():
            k = step - LAG_HIDDEN
            both = gown[lax.rem(k, OWN_RING)]
            for d in range(1, X):
                x_copy(k, d).wait_recv()
                both += xrecv[k, d - 1].astype(F32)
            gate = both[:, :fc]
            hid[k, rows(j, Q)] = (gate / (1.0 + jnp.exp(-gate)) * both[:, fc:]).astype(BF16)
            for d in range(1, X):
                h_x(k, d).start()
            h_mate(k, j).start()

        @pl.when((step >= LAG_FORWARD) & (step < K + LAG_FORWARD))
        def _():
            k = step - LAG_FORWARD
            for d in range(1, X):
                jj = x_at(d) * 2 + c
                h_mate(k, jj).wait_recv()
                h_mate(k, jj).start()

        @pl.when(step >= LAG_DOWN)
        def _():
            k = step - LAG_DOWN
            dw_copy(k).wait()
            for d in range(X):
                h_mate(k, x_at(d) * 2 + (1 - c)).wait_recv()
            acc[...] += jnp.dot(hid[k], dw[k], preferred_element_type=F32)

    def d_copy(d):
        return remote(
            dsend.at[rows(tp_at(d), R)], drecv.at[d - 1], d_send.at[d - 1], d_recv.at[d - 1],
            tp=tp_at(d),
        )

    dsend[...] = acc[...].astype(BF16)
    for d in range(1, n):
        d_copy(d).start()
    final = state[...] + acc[rows(t, R)]
    for d in range(1, n):
        d_copy(d).wait_recv()
        final += drecv[d - 1].astype(F32)
    fin[...] = final.reshape(s, r, W).astype(BF16)

    def f_copy(d):
        return remote(
            fin.at[sec_at(d)], outs.at[j], f_send.at[d - 1], f_recv.at[j], sec=sec_at(d)
        )

    def f_arrive(jj):
        return remote(fin.at[jj], outs.at[jj], f_send.at[0], f_recv.at[jj], sec=sec_at(1))

    for d in range(1, s):
        f_copy(d).start()
    outs[j] = fin[j]
    for d in range(1, s):
        f_arrive(sec_at(d)).wait_recv()
    for jj in range(s):
        out_ref[:, jj * W:(jj + 1) * W] = outs[jj]

    for d in range(1, n):
        a1(tp_at(d)).wait_send()
        nf_copy(d).wait_send()
        d_copy(d).wait_send()
    for d in range(1, s):
        sq_copy(d).wait_send()
        f_copy(d).wait_send()
    for d in range(n):
        tt = tp_at(d)
        for e in range(1, X):
            a2_x(tt, e, d == 0).wait_send()
            a2_mate(tt, x_at(e) * 2 + c).wait_send()
        a2_mate(tt, j, d == 0).wait_send()
    for i in range(NC):
        for d in range(1, n):
            rs_copy(i, d).wait_send()

    @pl.loop(0, K)
    def _(k):
        g_copy(k).wait_send()
        for d in range(1, X):
            x_copy(k, d).wait_send()
            h_x(k, d).wait_send()
            h_mate(k, x_at(d) * 2 + c).wait_send()
        h_mate(k, j).wait_send()


def layer(n, s, queries, lengths, slots, gain, keys, values, residual, out_weight, gate_weight, up_weight, down_weight):
    r, D = queries.shape
    P_, KW = keys.shape[1:]
    assert n % (KEY_VALUE_HEADS // 2) == 0
    X = s // 2
    R = s * r
    M = n * R
    Q = n * r
    C, W = out_weight.shape
    F = gate_weight.shape[1]
    K = pieces(F)
    fc = F // K
    NC = pieces(W)
    wc = W // NC
    XP = max(X - 1, 1)
    inside = fc % P_ == 0 and W % KW == 0 and K * (fc // P_) * (W // KW) >= 2 * r
    cache = (1, 16, 128) if inside else (2 * r, P_, KW)
    dma = pltpu.SemaphoreType.DMA
    vmem = pl.BlockSpec(memory_space=pltpu.VMEM)
    hbm = pl.BlockSpec(memory_space=pl.ANY)
    return pl.pallas_call(
        functools.partial(layer_kernel, n, s, r),
        out_shape=jax.ShapeDtypeStruct((r, D), BF16),
        in_specs=[vmem, pl.BlockSpec(memory_space=pltpu.SMEM), vmem, vmem] + [hbm] * 7,
        out_specs=vmem,
        scratch_shapes=[
            pltpu.VMEM((C, W), BF16),
            pltpu.VMEM((K, W, fc), BF16),
            pltpu.VMEM((K, W, fc), BF16),
            pltpu.VMEM((K, fc, W), BF16),
            pltpu.VMEM((r, D), BF16),
            pltpu.VMEM((r, QUERY_HEADS, HEAD_WIDTH), F32),
            pltpu.VMEM((r, 2 * QUERY_HEADS // KEY_VALUE_HEADS, HEAD_WIDTH), F32),
            pltpu.VMEM((n, s, r, C), BF16),
            pltpu.VMEM((M, C), BF16),
            pltpu.VMEM((NC, M, wc), F32),
            pltpu.VMEM((NC, M, wc), BF16),
            pltpu.VMEM((NC, n - 1, R, wc), BF16),
            pltpu.VMEM((R, W), F32),
            pltpu.VMEM((s, R, 128), F32),
            pltpu.VMEM((M, W), BF16),
            pltpu.VMEM((2, M, 2 * fc), F32),
            pltpu.VMEM((K, X, Q, 2 * fc), BF16),
            pltpu.VMEM((K, X, Q, 2 * fc), BF16),
            pltpu.VMEM((OWN_RING, Q, 2 * fc), F32),
            pltpu.VMEM((K, XP, Q, 2 * fc), BF16),
            pltpu.VMEM((K, XP, Q, 2 * fc), BF16),
            pltpu.VMEM((K, M, fc), BF16),
            pltpu.VMEM((M, W), F32),
            pltpu.VMEM((M, W), BF16),
            pltpu.VMEM((n - 1, R, W), BF16),
            pltpu.VMEM((s, r, W), BF16),
            pltpu.VMEM((s, r, W), BF16),
            pltpu.VMEM(cache, BF16),
            dma((KEY_VALUE_HEADS // 2, 2 * r)), dma,
            dma((4,)), dma((K,)), dma((K,)), dma((K,)), dma,
            dma((n,)), dma((n, s + XP)), dma((n, s)),
            dma((NC, n - 1)), dma((NC, n - 1)),
            dma((s - 1,)), dma((s,)),
            dma((n - 1,)), dma((n,)),
            dma((K,)), dma((K,)),
            dma((K, XP)), dma((K, XP)),
            dma((K, s + XP)), dma((K, s)),
            dma((n - 1,)), dma((n - 1,)),
            dma((s - 1,)), dma((s,)),
        ],
        compiler_params=pltpu.CompilerParams(
            collective_id=0, has_side_effects=True, vmem_limit_bytes=67043328
        ),
        name="layer",
    )(queries, lengths, slots, gain, keys, values, residual, out_weight, gate_weight, up_weight, down_weight)


def local(
    queries,
    keys,
    values,
    lengths,
    batch_of_slot,
    residual,
    out_weight,
    norm_gain,
    gate_weight,
    up_weight,
    down_weight,
):
    return layer(
        lax.axis_size("tp"), lax.axis_size("sec"), queries, lengths,
        batch_of_slot.reshape(1, -1), norm_gain.reshape(1, -1), keys, values, residual,
        out_weight, gate_weight, up_weight, down_weight,
    )


def solution(mesh):
    return jax.shard_map(
        local,
        mesh=mesh,
        in_specs=(
            P(("parts", "sec", "tp"), None),
            P(("parts", "sec", "tp"), None, None),
            P(("parts", "sec", "tp"), None, None),
            P(("parts", "sec", "tp")),
            P("parts"),
            P("parts", "sec"),
            P("tp", "sec"),
            P("sec"),
            P("sec", "tp"),
            P("sec", "tp"),
            P("tp", "sec"),
        ),
        out_specs=P(("parts", "sec", "tp"), None),
        check_vma=False,
    )
```
